32 devices in a mesh: row: 2 (over x), col: 8 (over z, y), layer: 2 (over core).
Axes of the slice: x: 2, y: 2, z: 4, core: 2. Of those that a mesh axis runs over, the one named last changes fastest.
Arguments:
- owned_blocks: bfloat16 [512, 32, 128, 128], P(('row', 'col', 'layer')), may hold values from -1 to 1
- slot_rows: int32 [512], P(('row', 'col', 'layer')), may hold values from -1 to 255, as said below
- block_cols: int32 [512, 32], P(('row', 'col', 'layer')), may hold values from 0 to 255, as said below
Outputs:
- product_blocks: bfloat16 [256, 32, 128, 128], P(('row', 'layer'), 'col')
The draws below stay inside these ranges and needn't reach their ends.
Inputs may be any that keep to these rules, and one draw needn't show every extreme that they name: `slot_rows`: every block row appears in exactly one slot. The 16 slots of the device at grid row r, grid column c and layer l (slots ((r * 8 + c) * 2 + l) * 16 onward) hold only block rows i with i // 128 = r and (i // 16) % 2 = l, or -1. In every grid row and layer some device uses all of its slots. block_cols[s, p] lies in panel p, between p * 8 and p * 8 + 7, also for unused slots.
All inputs are finite; a program needn't handle non-finite values.
Results may differ from the reference program's by a relative error of at most 0.001.
Values may be sent and summed in bfloat16 or wider, within the bound.
A program may use at most 256 MiB of HBM per device.

```python
import jax
import jax.numpy as jnp
from jax import lax

NB = 256
BLOCK_ORBITALS = 128
ROW_BLOCK_COUNT = 32
GRID_ROWS = 2
GRID_COLS = 8
LAYERS = 2
W = 8
HALF = 64
PPD = 2
OWN_CAP = 16
SLOT_COUNT = 512


def grid_order_rows_drawn():
    position = jnp.arange(NB, dtype=jnp.int32)
    group_index = position // HALF
    grid_row = group_index // LAYERS
    layer_index = group_index % LAYERS
    within = position % HALF
    upper_part = within // (PPD * W)
    inner_part = within // W % PPD
    offset = within % W
    panel_index = grid_row * (ROW_BLOCK_COUNT // GRID_ROWS) + upper_part * PPD * LAYERS + layer_index * PPD + inner_part
    return (panel_index * W + offset).astype(jnp.int32)


def local_pattern(pattern_key):
    row_index = jnp.arange(NB, dtype=jnp.int32)
    panels = jnp.arange(ROW_BLOCK_COUNT, dtype=jnp.int32)
    moves = jax.random.randint(pattern_key, (NB, ROW_BLOCK_COUNT), -1, 2, dtype=jnp.int32)
    offsets = (row_index[:, None] % W + moves) % W
    own_panel = (row_index // W)[:, None] == panels[None, :]
    offsets = jnp.where(own_panel, row_index[:, None] % W, offsets)
    return (panels[None, :] * W + offsets).astype(jnp.int32)


def one_group(group_key, group_rows):
    first_key, later_random_key, third_key = jax.random.split(group_key, 3)
    shuffled = group_rows[jax.random.permutation(first_key, HALF)]
    full_owner = jax.random.randint(later_random_key, (), 0, GRID_COLS, dtype=jnp.int32)
    others = jax.random.permutation(third_key, (GRID_COLS - 1) * OWN_CAP).astype(jnp.int32)[:HALF - OWN_CAP]
    owner_col = others // OWN_CAP
    owner_col = owner_col + (owner_col >= full_owner).astype(jnp.int32)
    slot_index = jnp.concatenate([full_owner * OWN_CAP + jnp.arange(OWN_CAP, dtype=jnp.int32), owner_col * OWN_CAP + others % OWN_CAP])
    return jnp.full((GRID_COLS * OWN_CAP,), -1, jnp.int32).at[slot_index].set(shuffled)


def owner_table(owner_key):
    grid_rows = grid_order_rows_drawn().reshape(GRID_ROWS * LAYERS, HALF)
    group_keys = jax.random.split(owner_key, GRID_ROWS * LAYERS)
    lookup_tables = jax.vmap(one_group)(group_keys, grid_rows)
    lookup_tables = lookup_tables.reshape(GRID_ROWS, LAYERS, GRID_COLS, OWN_CAP).transpose(0, 2, 1, 3)
    return lookup_tables.reshape(SLOT_COUNT)


def draw_slot_rows(key, part):
    return owner_table(jax.random.fold_in(key, 11))


def draw_block_cols(key, part):
    slot_table = owner_table(jax.random.fold_in(key, 11))
    pattern = local_pattern(jax.random.fold_in(key, 12))
    return pattern[jnp.maximum(slot_table, 0)]


def draw_owned_blocks(key, part):
    spread_scale = float(BLOCK_ORBITALS * ROW_BLOCK_COUNT) ** (-0.25)
    complete_shape = (SLOT_COUNT, ROW_BLOCK_COUNT, BLOCK_ORBITALS, BLOCK_ORBITALS)
    values = jnp.clip(jax.random.normal(key, complete_shape, jnp.float32), -4.0, 4.0)
    return (values * spread_scale).astype(jnp.bfloat16)


def setup_inputs(seed: int = 0) -> dict:
    arg_keys = jax.random.split(jax.random.key(seed), 4)
    owned_blocks = draw_owned_blocks(jax.random.fold_in(arg_keys[3], 71), 0)
    slot_rows = draw_slot_rows(jax.random.fold_in(arg_keys[3], 71), 0)
    block_cols = draw_block_cols(jax.random.fold_in(arg_keys[3], 71), 0)
    return dict(owned_blocks=owned_blocks, slot_rows=slot_rows, block_cols=block_cols)


def grid_order_rows():
    position = jnp.arange(NB, dtype=jnp.int32)
    group_index = position // HALF
    grid_row = group_index // LAYERS
    layer_index = group_index % LAYERS
    within = position % HALF
    upper_part = within // (PPD * W)
    inner_part = (within // W) % PPD
    offset = within % W
    panel_index = grid_row * (ROW_BLOCK_COUNT // GRID_ROWS) + upper_part * PPD * LAYERS + layer_index * PPD + inner_part
    return (panel_index * W + offset).astype(jnp.int32)


def reference(owned_blocks, slot_rows, block_cols):
    target = jnp.where(slot_rows >= 0, slot_rows, NB).astype(jnp.int32)
    blocks = jnp.zeros((NB, ROW_BLOCK_COUNT, BLOCK_ORBITALS, BLOCK_ORBITALS), owned_blocks.dtype).at[target].set(owned_blocks, mode="drop")
    columns = jnp.zeros((NB, ROW_BLOCK_COUNT), jnp.int32).at[target].set(block_cols.astype(jnp.int32), mode="drop")

    def one_row(row_index):
        row_columns = columns[row_index]
        left_blocks = blocks[row_index].astype(jnp.float32)
        partner = blocks[row_columns].astype(jnp.float32)
        partner_cols = columns[row_columns]
        matched = (partner_cols == row_columns[None, :]).astype(jnp.float32)
        partner = partner * matched[:, :, None, None]
        summed = jnp.einsum("tab,tsbc->sac", left_blocks, partner)
        return summed.astype(jnp.bfloat16)

    grid_order = grid_order_rows()
    return lax.map(one_row, grid_order)
```

```python
import functools

import jax
import jax.numpy as jnp
from jax import lax
from jax.experimental import pallas as pl
from jax.experimental.pallas import tpu as pltpu
from jax.sharding import PartitionSpec as P

MESH = pl.DeviceIdType.MESH
NB = 256
GROUP = 4


def square_kernel(
    rows, cols, layers, outer, parts, index_ref, code_ref, owned_ref, out_ref, left_ref,
    land_ref, *scratch,
):
    width, _, height = left_ref.shape[:3]
    slots = owned_ref.shape[0]
    panels = cols * width
    nb = rows * layers * height
    tables = scratch[:width]
    (
        got, sums, a_buf, o_buf, swap_send, swap_recv, send_sem, recv_sem, row_send,
        layer_send, table_recv, own_sem, got_sem, a_sem, o_sem,
    ) = scratch[width:]
    inner = cols // outer
    my_row, my_col, my_layer = (lax.axis_index(a) for a in ("row", "col", "layer"))
    my_outer, my_inner = my_col // inner, lax.rem(my_col, inner)
    my_group = my_row * layers + my_layer

    row_peers = [lax.rem(my_row + d, rows) for d in range(1, rows)]
    layer_peers = [lax.rem(my_layer + d, layers) for d in range(1, layers)]
    col_peers = [lax.rem(my_col + d, cols) for d in range(1, cols)]
    col_givers = [lax.rem(my_col + cols - d, cols) for d in range(1, cols)]
    barrier = pltpu.get_barrier_semaphore()
    for axis, peers in (("col", col_peers), ("row", row_peers), ("layer", layer_peers)):
        for peer in peers:
            pl.semaphore_signal(barrier, inc=1, device_id={axis: peer}, device_id_type=MESH)
    pl.semaphore_wait(barrier, rows + cols + layers - 3)

    def swap(q, d):
        return pltpu.make_async_remote_copy(
            src_ref=owned_ref.at[:, col_peers[d - 1] * width + q],
            dst_ref=land_ref.at[q, pl.ds(my_col * slots, slots)],
            send_sem=swap_send.at[q, d],
            recv_sem=swap_recv.at[q, my_col],
            device_id={"col": col_peers[d - 1]},
            device_id_type=MESH,
        )

    def keep(q):
        return pltpu.make_async_copy(
            owned_ref.at[:, my_col * width + q],
            land_ref.at[q, pl.ds(my_col * slots, slots)],
            swap_send.at[q, 0],
        )

    def wait_swap(q):
        keep(q).wait()
        for giver in col_givers:
            place = land_ref.at[q, pl.ds(giver * slots, slots)]
            pltpu.make_async_remote_copy(
                src_ref=place,
                dst_ref=place,
                send_sem=swap_send.at[q, 1],
                recv_sem=swap_recv.at[q, giver],
                device_id={"col": giver},
                device_id_type=MESH,
            ).wait_recv()

    lines = (
        (my_outer + 1 < outer, {"col": my_col + inner}),
        (my_outer >= 1, {"col": my_col - inner}),
        (my_inner + 1 < inner, {"col": my_col + 1}),
        (my_inner >= 1, {"col": my_col - 1}),
    )
    ending = []

    def send_left(q, kind, item, way, condition, own=False):
        start, size, _ = parts[kind]

        def make():
            place = left_ref.at[q, item, pl.ds(start, size)]
            source = tables[q].at[pl.ds(my_group * height + start, size)] if own else place
            return pltpu.make_async_remote_copy(
                src_ref=source,
                dst_ref=place,
                send_sem=send_sem.at[q, kind, item, way],
                recv_sem=recv_sem.at[q, kind, item],
                device_id=lines[way][1],
                device_id_type=MESH,
            )

        condition = jnp.logical_and(condition, lines[way][0])

        @pl.when(condition)
        def _():
            make().start()

        ending.append((condition, make))

    def wait_left(q, kind, item, condition):
        start, size, _ = parts[kind]

        @pl.when(condition)
        def _():
            place = left_ref.at[q, item, pl.ds(start, size)]
            pltpu.make_async_remote_copy(
                src_ref=place,
                dst_ref=place,
                send_sem=send_sem.at[q, kind, item, 0],
                recv_sem=recv_sem.at[q, kind, item],
                device_id={"col": my_col},
                device_id_type=MESH,
            ).wait_recv()

    always = my_col >= 0
    axes = (
        (outer, inner, my_outer, (0, 1)),
        (inner, 1, my_inner, (2, 3)),
    )

    def stages(q, kind, first, second):
        size1, stride1, me1, ways1 = first
        size2, stride2, me2, ways2 = second

        def own():
            for way in ways1 + ways2:
                send_left(q, kind, my_col, way, always, own=True)

        def along_first(step):
            for sign, way in ((-1, ways1[0]), (1, ways1[1])):
                at = me1 + sign * step
                there = at >= 0 if sign < 0 else at < size1
                item = at * stride1 + me2 * stride2
                wait_left(q, kind, item, there)
                for onward in (way,) + ways2:
                    send_left(q, kind, item, onward, there)

        def along_second(step):
            for sign, way in ((-1, ways2[0]), (1, ways2[1])):
                at = me2 + sign * step
                there = at >= 0 if sign < 0 else at < size2
                for other in range(size1):
                    item = other * stride1 + at * stride2
                    wait_left(q, kind, item, there)
                    send_left(q, kind, item, way, there)

        return (
            [own]
            + [functools.partial(along_first, s) for s in range(1, size1)]
            + [functools.partial(along_second, s) for s in range(1, size2)]
        )

    plans = [
        [
            stages(q, kind, *(axes if part[2] else axes[::-1]))
            for kind, part in enumerate(parts)
        ]
        for q in range(width)
    ]
    depth = len(plans[0][0])

    def table_copy(q, group, sem, device):
        place = tables[q].at[pl.ds(group * height, height)]
        return pltpu.make_async_remote_copy(
            src_ref=place,
            dst_ref=place,
            send_sem=sem,
            recv_sem=table_recv.at[q, group],
            device_id=device,
            device_id_type=MESH,
        )

    def row_copy(q, d):
        return table_copy(q, my_group, row_send.at[q, d], {"row": row_peers[d]})

    def layer_copy(q, d, row):
        group = row * layers + my_layer
        return table_copy(q, group, layer_send.at[q, d, row], {"layer": layer_peers[d]})

    def wait_table(q, group):
        table_copy(q, group, row_send.at[q, 0], {"row": my_row}).wait_recv()

    def own_left(q):
        return pltpu.make_async_copy(
            tables[q].at[pl.ds(my_group * height, height)], left_ref.at[q, my_col], own_sem.at[q]
        )

    def arrive(q):
        wait_swap(q)
        fetch = pltpu.make_async_copy(land_ref.at[q], got, got_sem)
        fetch.start()
        fetch.wait()

        def pick(t, carry):
            tables[q][my_group * height + t] = got[index_ref[t]]
            return carry

        lax.fori_loop(0, height, pick, 0)
        for plan in plans[q]:
            plan[0]()
        for d in range(rows - 1):
            row_copy(q, d).start()
        for d in range(layers - 1):
            layer_copy(q, d, my_row).start()
        own_left(q).start()

    def gather(q, stage):
        for plan in plans[q]:
            plan[stage]()
        if stage == 1:
            for peer in row_peers:
                wait_table(q, peer * layers + my_layer)
                for d in range(layers - 1):
                    layer_copy(q, d, peer).start()

    count = height // GROUP

    def multiply(q, first, last):
        own_left(q).wait()

        def fetch(i, slot):
            return pltpu.make_async_copy(
                left_ref.at[q, :, pl.ds(i * GROUP, GROUP)], a_buf.at[slot], a_sem.at[slot]
            )

        def put(i, slot):
            return pltpu.make_async_copy(
                o_buf.at[slot], out_ref.at[pl.ds(i * GROUP, GROUP)], o_sem.at[slot]
            )

        fetch(0, 0).start()

        def some_rows(i, carry):
            slot = lax.rem(i, 2)

            @pl.when(i + 1 < count)
            def _():
                fetch(i + 1, 1 - slot).start()

            if last:

                @pl.when(i >= 2)
                def _():
                    put(i - 2, slot).wait()

            fetch(i, slot).wait()

            def one_row(g, carry):
                t = i * GROUP + g
                lefts = jnp.concatenate([a_buf[slot, c, g] for c in range(cols)], axis=1)
                for j in range(width):
                    start = (t * width + j) * panels + q
                    rights = [tables[j][code_ref[start + c * width]] for c in range(cols)]
                    term = jnp.dot(
                        lefts,
                        jnp.concatenate(rights, axis=0),
                        preferred_element_type=jnp.float32,
                    )
                    if not first:
                        term = sums[t, j] + term
                    if last:
                        o_buf[slot, g, j] = term.astype(o_buf.dtype)
                    else:
                        sums[t, j] = term
                return carry

            lax.fori_loop(0, GROUP, one_row, 0)
            if last:
                put(i, slot).start()
            return carry

        lax.fori_loop(0, count, some_rows, 0)
        if last:
            for i in range(max(count - 2, 0), count):
                put(i, i % 2).wait()

    for q in range(width):
        keep(q).start()
        for d in range(1, cols):
            swap(q, d).start()
    for q in range(width):
        tables[q][nb] = jnp.zeros_like(tables[q][nb])

    done = 0
    for turn in range(2 * (width - 1) + depth):
        for q in range(width):
            stage = turn - 2 * q if turn < 2 * width else turn - 2 * q
            if stage == 0:
                arrive(q)
            elif 0 < stage < depth:
                gather(q, stage)
        if turn == 2 * (width - 1) + 1:
            for q in range(width):
                for layer_peer in layer_peers:
                    for row in range(rows):
                        wait_table(q, row * layers + layer_peer)
        if turn > 2 * (width - 1):
            while done < width - 1 and turn - 2 * done >= depth - 1:
                multiply(done, done == 0, False)
                done += 1
    while done < width:
        multiply(done, done == 0, done == width - 1)
        done += 1

    for condition, make in ending:

        @pl.when(condition)
        def _(make=make):
            make().wait_send()

    for q in range(width):
        for d in range(1, cols):
            swap(q, d).wait_send()
        for d in range(rows - 1):
            row_copy(q, d).wait_send()
        for d in range(layers - 1):
            for row in [my_row] + row_peers:
                layer_copy(q, d, row).wait_send()


def square(index, codes, owned, rows, cols, layers, height):
    slots, panels, size, _ = owned.shape
    width = panels // cols
    nb = rows * layers * height
    outer = 4 if cols % 4 == 0 else 1
    swapped = max(height * 6 // 64, 1)
    middle = (height + swapped) // 2
    parts = (
        (0, swapped, False),
        (swapped, middle - swapped, True),
        (middle, height - middle, True),
    )
    kinds = len(parts)
    kind = owned.dtype
    scratch = [pltpu.VMEM((nb + 1, size, size), kind) for _ in range(width)] + [
        pltpu.VMEM((cols * slots, size, size), kind),
        pltpu.VMEM((height, width, size, size), jnp.float32),
        pltpu.VMEM((2, cols, GROUP, size, size), kind),
        pltpu.VMEM((2, GROUP, width, size, size), kind),
    ]
    need = sum(s.shape[0] * jnp.dtype(s.dtype).itemsize * (
        functools.reduce(lambda a, b: a * b, s.shape[1:])) for s in scratch)
    anywhere = pl.BlockSpec(memory_space=pl.ANY)
    return pl.pallas_call(
        functools.partial(square_kernel, rows, cols, layers, outer, parts),
        out_shape=(
            jax.ShapeDtypeStruct((height, width, size, size), kind),
            jax.ShapeDtypeStruct((width, cols, height, size, size), kind),
            jax.ShapeDtypeStruct((width, cols * slots, size, size), kind),
        ),
        in_specs=[pl.BlockSpec(memory_space=pltpu.SMEM)] * 2 + [anywhere],
        out_specs=(anywhere,) * 3,
        scratch_shapes=scratch + [
            pltpu.SemaphoreType.DMA((width, cols)),
            pltpu.SemaphoreType.DMA((width, cols)),
            pltpu.SemaphoreType.DMA((width, kinds, cols, 4)),
            pltpu.SemaphoreType.DMA((width, kinds, cols)),
            pltpu.SemaphoreType.DMA((width, max(rows - 1, 1))),
            pltpu.SemaphoreType.DMA((width, max(layers - 1, 1), rows)),
            pltpu.SemaphoreType.DMA((width, rows * layers)),
            pltpu.SemaphoreType.DMA((width,)),
            pltpu.SemaphoreType.DMA,
            pltpu.SemaphoreType.DMA((2,)),
            pltpu.SemaphoreType.DMA((2,)),
        ],
        compiler_params=pltpu.CompilerParams(
            collective_id=0, has_side_effects=True, vmem_limit_bytes=need + (4 << 20)
        ),
        cost_estimate=pl.CostEstimate(
            flops=2 * height * panels * width * size**3, bytes_accessed=1 << 28, transcendentals=0
        ),
        name="square",
    )(index, codes, owned)[0]


def shards(owned_blocks, slot_rows, block_cols):
    own_slots, panels, size, _ = owned_blocks.shape
    rows = lax.axis_size("row")
    cols = lax.axis_size("col")
    layers = lax.axis_size("layer")
    width = panels // cols
    slots = own_slots * rows * cols * layers
    my_row, my_col, my_layer = (lax.axis_index(a) for a in ("row", "col", "layer"))
    my_group = my_row * layers + my_layer

    ids = jnp.concatenate([slot_rows[:, None], block_cols], axis=1)
    ids = lax.all_gather(ids, ("row", "col", "layer"), axis=0, tiled=True)
    nb = NB
    per_layer = panels // (cols * layers) * (nb // panels)
    height = nb // (rows * layers)
    place = jnp.arange(nb, dtype=jnp.int32)
    part, within = place // height, place % height
    row_at = (
        part // layers * (nb // rows)
        + within // per_layer * per_layer * layers
        + part % layers * per_layer
        + within % per_layer
    )
    holds = ids[None, :, 0] == row_at[:, None]
    slot_at = jnp.sum(
        jnp.where(holds, jnp.arange(slots, dtype=jnp.int32)[None, :], 0), axis=1
    )
    my_slots = lax.dynamic_slice_in_dim(slot_at, my_group * height, height)
    owner = my_slots // own_slots // layers % cols
    index = owner * own_slots + my_slots % own_slots

    columns = jnp.dot(
        holds.astype(jnp.float32),
        ids[:, 1:].astype(jnp.float32),
        precision=lax.Precision.HIGHEST,
    ).astype(jnp.int32)
    mine = lax.dynamic_slice_in_dim(columns, my_group * height, height)
    wanted = lax.dynamic_slice_in_dim(mine, my_col * width, width, 1)
    inside = mine % (nb // rows)
    partner = (
        (mine // (nb // rows) * layers + inside // per_layer % layers) * height
        + inside // (per_layer * layers) * per_layer
        + inside % per_layer
    )
    reach = lax.dynamic_slice_in_dim(columns, my_col * width, width, 1)
    matched = reach[partner] == wanted[:, None, :]
    codes = jnp.where(matched, partner[:, :, None], nb).transpose(0, 2, 1)
    return square(index, codes.reshape(-1), owned_blocks, rows, cols, layers, height)


def solution(mesh):
    return jax.shard_map(
        shards,
        mesh=mesh,
        in_specs=(
            P(("row", "col", "layer"), None, None, None),
            P(("row", "col", "layer")),
            P(("row", "col", "layer"), None),
        ),
        out_specs=P(("row", "layer"), "col", None, None),
        check_vma=False,
    )
```

```python
import functools

import jax
import jax.numpy as jnp
from jax import lax
from jax.experimental import pallas as pl
from jax.experimental.pallas import tpu as pltpu
from jax.sharding import PartitionSpec as P

MESH = pl.DeviceIdType.MESH
NB = 256
GROUP = 4
FIRST = 64
CUT = 1
SHARE = (1, 1, 1, 1, 1)
EARLY = 3
STRAIGHT = 3


def meet_kernel(rows, cols, layers, mine_ref, all_ref, send_sem, recv_sem):
    my_row, my_col, my_layer = (lax.axis_index(a) for a in ("row", "col", "layer"))
    row_peers = [lax.rem(my_row + d, rows) for d in range(1, rows)]
    col_peers = [lax.rem(my_col + d, cols) for d in range(1, cols)]
    layer_peers = [lax.rem(my_layer + d, layers) for d in range(1, layers)]
    barrier = pltpu.get_barrier_semaphore()
    for axis, peers in (("col", col_peers), ("row", row_peers), ("layer", layer_peers)):
        for peer in peers:
            pl.semaphore_signal(barrier, inc=1, device_id={axis: peer}, device_id_type=MESH)
    all_ref[my_row, my_col, my_layer] = mine_ref[...]
    pl.semaphore_wait(barrier, rows + cols + layers - 3)
    steps = (
        ("layer", layer_peers, my_layer, lambda at: all_ref.at[my_row, my_col, at]),
        ("row", row_peers, my_row, lambda at: all_ref.at[at, my_col]),
        ("col", col_peers, my_col, lambda at: all_ref.at[:, at]),
    )
    sent = 0
    for axis, peers, me, place in steps:

        def copy(n, peer, at, place=place, axis=axis, base=sent):
            return pltpu.make_async_remote_copy(
                src_ref=place(at),
                dst_ref=place(at),
                send_sem=send_sem.at[base + n],
                recv_sem=recv_sem.at[base + n],
                device_id={axis: peer},
                device_id_type=MESH,
            )

        copies = [copy(n, peer, me) for n, peer in enumerate(peers)]
        for one in copies:
            one.start()
        size = len(peers) + 1
        for n in range(len(peers)):
            copy(n, peers[n], lax.rem(me + size - n - 1, size)).wait_recv()
        for one in copies:
            one.wait_send()
        sent += len(peers)


def meet(mine, rows, cols, layers):
    count = rows + cols + layers - 3
    return pl.pallas_call(
        functools.partial(meet_kernel, rows, cols, layers),
        out_shape=jax.ShapeDtypeStruct((rows, cols, layers) + mine.shape, mine.dtype),
        in_specs=[pl.BlockSpec(memory_space=pltpu.VMEM)],
        out_specs=pl.BlockSpec(memory_space=pltpu.VMEM),
        scratch_shapes=[
            pltpu.SemaphoreType.DMA((count,)),
            pltpu.SemaphoreType.DMA((count,)),
        ],
        compiler_params=pltpu.CompilerParams(collective_id=1, has_side_effects=True),
        name="meet",
    )(mine)


def square_kernel(
    rows, cols, layers, outer, parts, chunks, index_ref, code_ref, owned_ref, first_ref,
    out_ref, left_ref, land_ref, *scratch,
):
    width, _, height = left_ref.shape[:3]
    slots = owned_ref.shape[0]
    panels = cols * width
    nb = rows * layers * height
    tables = scratch[:width]
    (
        got, sums, a_buf, o_buf, swap_send, swap_recv, send_sem, recv_sem, row_send,
        layer_send, table_recv, own_sem, got_sem, a_sem, o_sem,
    ) = scratch[width:]
    inner = cols // outer
    my_row, my_col, my_layer = (lax.axis_index(a) for a in ("row", "col", "layer"))
    my_outer, my_inner = my_col // inner, lax.rem(my_col, inner)
    my_group = my_row * layers + my_layer

    row_peers = [lax.rem(my_row + d, rows) for d in range(1, rows)]
    layer_peers = [lax.rem(my_layer + d, layers) for d in range(1, layers)]
    col_peers = [lax.rem(my_col + d, cols) for d in range(1, cols)]
    col_givers = [lax.rem(my_col + cols - d, cols) for d in range(1, cols)]
    barrier = pltpu.get_barrier_semaphore()
    for axis, peers in (("col", col_peers), ("row", row_peers), ("layer", layer_peers)):
        for peer in peers:
            pl.semaphore_signal(barrier, inc=1, device_id={axis: peer}, device_id_type=MESH)
    pl.semaphore_wait(barrier, rows + cols + layers - 3)

    def swap(n, d):
        q, low, tall = chunks[n]
        return pltpu.make_async_remote_copy(
            src_ref=owned_ref.at[:, col_peers[d - 1] * width + q, pl.ds(low, tall)],
            dst_ref=land_ref.at[q, pl.ds(my_col * slots, slots), pl.ds(low, tall)],
            send_sem=swap_send.at[n, d],
            recv_sem=swap_recv.at[n, my_col],
            device_id={"col": col_peers[d - 1]},
            device_id_type=MESH,
        )

    def keep(n):
        q, low, tall = chunks[n]
        return pltpu.make_async_copy(
            owned_ref.at[:, my_col * width + q, pl.ds(low, tall)],
            land_ref.at[q, pl.ds(my_col * slots, slots), pl.ds(low, tall)],
            swap_send.at[n, 0],
        )

    def start_swap(n):
        if n < len(chunks):
            keep(n).start()
            for d in range(1, cols):
                swap(n, d).start()

    def wait_swap(n):
        q, low, tall = chunks[n]
        keep(n).wait()
        for giver in col_givers:
            place = land_ref.at[q, pl.ds(giver * slots, slots), pl.ds(low, tall)]
            pltpu.make_async_remote_copy(
                src_ref=place,
                dst_ref=place,
                send_sem=swap_send.at[n, 1],
                recv_sem=swap_recv.at[n, giver],
                device_id={"col": giver},
                device_id_type=MESH,
            ).wait_recv()

    lines = (
        (my_outer + 1 < outer, {"col": my_col + inner}),
        (my_outer >= 1, {"col": my_col - inner}),
        (my_inner + 1 < inner, {"col": my_col + 1}),
        (my_inner >= 1, {"col": my_col - 1}),
    )
    ending = []

    def left_place(n, kind, item):
        q, low, tall = chunks[n]
        start, size, _ = parts[n][kind]
        return left_ref.at[q, item, pl.ds(start, size), pl.ds(low, tall)]

    def send_left(n, kind, item, way, condition, own=False):
        q, low, tall = chunks[n]
        start, size, _ = parts[n][kind]

        def make():
            place = left_place(n, kind, item)
            source = place
            if own:
                source = tables[q].at[pl.ds(my_group * height + start, size), pl.ds(low, tall)]
            return pltpu.make_async_remote_copy(
                src_ref=source,
                dst_ref=place,
                send_sem=send_sem.at[n, kind, item, way],
                recv_sem=recv_sem.at[n, kind, item],
                device_id=lines[way][1],
                device_id_type=MESH,
            )

        condition = jnp.logical_and(condition, lines[way][0])

        @pl.when(condition)
        def _():
            make().start()

        ending.append((condition, make))

    def wait_left(n, kind, item, condition):
        @pl.when(condition)
        def _():
            place = left_place(n, kind, item)
            pltpu.make_async_remote_copy(
                src_ref=place,
                dst_ref=place,
                send_sem=send_sem.at[n, kind, item, 0],
                recv_sem=recv_sem.at[n, kind, item],
                device_id={"col": my_col},
                device_id_type=MESH,
            ).wait_recv()

    always = my_col >= 0
    axes = (
        (outer, inner, my_outer, (0, 1)),
        (inner, 1, my_inner, (2, 3)),
    )

    def stages(n, kind, first, second):
        size1, stride1, me1, ways1 = first
        size2, stride2, me2, ways2 = second

        def own():
            for way in ways1 + ways2:
                send_left(n, kind, my_col, way, always, own=True)

        def along_first(step):
            for sign, way in ((-1, ways1[0]), (1, ways1[1])):
                at = me1 + sign * step
                there = at >= 0 if sign < 0 else at < size1
                item = at * stride1 + me2 * stride2
                wait_left(n, kind, item, there)
                for onward in (way,) + ways2:
                    send_left(n, kind, item, onward, there)

        def along_second(step):
            for sign, way in ((-1, ways2[0]), (1, ways2[1])):
                at = me2 + sign * step
                there = at >= 0 if sign < 0 else at < size2
                for other in range(size1):
                    item = other * stride1 + at * stride2
                    wait_left(n, kind, item, there)
                    send_left(n, kind, item, way, there)

        return (
            [own]
            + [functools.partial(along_first, s) for s in range(1, size1)]
            + [functools.partial(along_second, s) for s in range(1, size2)]
        )

    plans = [
        [
            stages(n, kind, *(axes if part[2] else axes[::-1]))
            for kind, part in enumerate(parts[n])
        ]
        for n in range(len(chunks))
    ]
    depth = len(plans[0][0])

    def table_copy(n, group, sem, device):
        q, low, tall = chunks[n]
        place = tables[q].at[pl.ds(group * height, height), pl.ds(low, tall)]
        return pltpu.make_async_remote_copy(
            src_ref=place,
            dst_ref=place,
            send_sem=sem,
            recv_sem=table_recv.at[n, group],
            device_id=device,
            device_id_type=MESH,
        )

    def row_copy(n, d):
        return table_copy(n, my_group, row_send.at[n, d], {"row": row_peers[d]})

    def layer_copy(n, d, row):
        group = row * layers + my_layer
        return table_copy(n, group, layer_send.at[n, d, row], {"layer": layer_peers[d]})

    def wait_table(n, group):
        table_copy(n, group, row_send.at[n, 0], {"row": my_row}).wait_recv()

    def own_left(n):
        q, low, tall = chunks[n]
        return pltpu.make_async_copy(
            tables[q].at[pl.ds(my_group * height, height), pl.ds(low, tall)],
            left_ref.at[q, my_col, :, pl.ds(low, tall)],
            own_sem.at[n],
        )

    def arrive(n):
        q, low, tall = chunks[n]
        source = first_ref
        if n:
            wait_swap(n)
            source = land_ref.at[q, :, pl.ds(low, tall)]
            start_swap(n + 1)
        fetch = pltpu.make_async_copy(source, got.at[:, pl.ds(low, tall)], got_sem)
        fetch.start()
        fetch.wait()

        def pick(t, carry):
            tables[q][my_group * height + t, pl.ds(low, tall)] = got[index_ref[t], pl.ds(low, tall)]
            return carry

        lax.fori_loop(0, height, pick, 0)
        for plan in plans[n]:
            plan[0]()
        for d in range(rows - 1):
            row_copy(n, d).start()
        for d in range(layers - 1):
            layer_copy(n, d, my_row).start()
        own_left(n).start()

    def gather(n, stage):
        for plan in plans[n]:
            plan[stage]()
        if stage == 1:
            for peer in row_peers:
                wait_table(n, peer * layers + my_layer)
                for d in range(layers - 1):
                    layer_copy(n, d, peer).start()

    def fetch(q, i, slot):
        return pltpu.make_async_copy(
            left_ref.at[q, :, pl.ds(i * GROUP, GROUP)], a_buf.at[slot], a_sem.at[slot]
        )

    def put(i, slot):
        return pltpu.make_async_copy(
            o_buf.at[slot], out_ref.at[pl.ds(i * GROUP, GROUP)], o_sem.at[slot]
        )

    def multiply(q, low, high):
        first, last = q == 0, q == width - 1
        low, high = low // GROUP, high // GROUP
        fetch(q, low, low % 2).start()

        def some_rows(i, carry):
            slot = lax.rem(i, 2)

            @pl.when(i + 1 < high)
            def _():
                fetch(q, i + 1, 1 - slot).start()

            if last:

                @pl.when(i >= 2)
                def _():
                    put(i - 2, slot).wait()

            fetch(q, i, slot).wait()

            def one_row(g, carry):
                t = i * GROUP + g
                lefts = jnp.concatenate([a_buf[slot, c, g] for c in range(cols)], axis=1)
                for j in range(width):
                    start = (t * width + j) * panels + q
                    rights = [tables[j][code_ref[start + c * width]] for c in range(cols)]
                    term = jnp.dot(
                        lefts,
                        jnp.concatenate(rights, axis=0),
                        preferred_element_type=jnp.float32,
                    )
                    if not first:
                        term = sums[t, j] + term
                    if last:
                        o_buf[slot, g, j] = term.astype(o_buf.dtype)
                    else:
                        sums[t, j] = term
                return carry

            lax.fori_loop(0, GROUP, one_row, 0)
            if last:
                put(i, slot).start()
            return carry

        lax.fori_loop(low, high, some_rows, 0)

    start_swap(1)
    for q in range(width):
        tables[q][nb] = jnp.zeros_like(tables[q][nb])

    ready = {q: max(n for n, chunk in enumerate(chunks) if chunk[0] == q) for q in range(width)}
    final = len(chunks) - 1
    done = 0
    for turn in range(final + depth - 1):
        for n in range(len(chunks)):
            stage = turn - n
            if stage == 0:
                arrive(n)
            elif 0 < stage < depth:
                gather(n, stage)
        if turn == final + 1:
            for n in range(len(chunks)):
                for layer_peer in layer_peers:
                    for row in range(rows):
                        wait_table(n, row * layers + layer_peer)
                own_left(n).wait()
        if turn > final:
            while done < width - 1 and turn - ready[done] >= depth - 1:
                multiply(done, 0, height)
                done += 1
    while done < width - 1:
        multiply(done, 0, height)
        done += 1
    for kind, (start, size, _) in enumerate(parts[final]):
        plans[final][kind][depth - 1]()
        multiply(width - 1, start, start + size)
    for i in range(max(height // GROUP - 2, 0), height // GROUP):
        put(i, i % 2).wait()

    for condition, make in ending:

        @pl.when(condition)
        def _(make=make):
            make().wait_send()

    for n in range(len(chunks)):
        if n:
            for d in range(1, cols):
                swap(n, d).wait_send()
        for d in range(rows - 1):
            row_copy(n, d).wait_send()
        for d in range(layers - 1):
            for row in [my_row] + row_peers:
                layer_copy(n, d, row).wait_send()


def square(index, codes, owned, first, rows, cols, layers, height):
    slots, panels, size, _ = owned.shape
    width = panels // cols
    nb = rows * layers * height
    outer = 4 if cols % 4 == 0 else 1
    tall = first.shape[1]
    chunks = [(0, low, tall) for low in range(0, size, tall)]
    step = size // CUT
    chunks += [(q, low, step) for q in range(1, width) for low in range(0, size, step)]
    pieces = len(chunks)
    blocks = height // GROUP
    parts = []
    for n in range(pieces):
        share = SHARE[n * len(SHARE) // pieces]
        straight = STRAIGHT if n == pieces - 1 else EARLY
        swapped = blocks * share // 16
        cuts = [swapped + (blocks - swapped) * k // straight for k in range(straight + 1)]
        parts.append(((0, swapped * GROUP, False),) * (swapped > 0) + tuple(
            (lo * GROUP, (hi - lo) * GROUP, True) for lo, hi in zip(cuts, cuts[1:])
        ))
    kinds = max(len(part) for part in parts)
    kind = owned.dtype
    scratch = [pltpu.VMEM((nb + 1, size, size), kind) for _ in range(width)] + [
        pltpu.VMEM((cols * slots, size, size), kind),
        pltpu.VMEM((height, width, size, size), jnp.float32),
        pltpu.VMEM((2, cols, GROUP, size, size), kind),
        pltpu.VMEM((2, GROUP, width, size, size), kind),
    ]
    need = sum(s.shape[0] * jnp.dtype(s.dtype).itemsize * (
        functools.reduce(lambda a, b: a * b, s.shape[1:])) for s in scratch)
    anywhere = pl.BlockSpec(memory_space=pl.ANY)
    return pl.pallas_call(
        functools.partial(square_kernel, rows, cols, layers, outer, tuple(parts), tuple(chunks)),
        out_shape=(
            jax.ShapeDtypeStruct((height, width, size, size), kind),
            jax.ShapeDtypeStruct((width, cols, height, size, size), kind),
            jax.ShapeDtypeStruct((width, cols * slots, size, size), kind),
        ),
        in_specs=[pl.BlockSpec(memory_space=pltpu.SMEM)] * 2 + [anywhere] * 2,
        out_specs=(anywhere,) * 3,
        scratch_shapes=scratch + [
            pltpu.SemaphoreType.DMA((pieces, cols)),
            pltpu.SemaphoreType.DMA((pieces, cols)),
            pltpu.SemaphoreType.DMA((pieces, kinds, cols, 4)),
            pltpu.SemaphoreType.DMA((pieces, kinds, cols)),
            pltpu.SemaphoreType.DMA((pieces, max(rows - 1, 1))),
            pltpu.SemaphoreType.DMA((pieces, max(layers - 1, 1), rows)),
            pltpu.SemaphoreType.DMA((pieces, rows * layers)),
            pltpu.SemaphoreType.DMA((pieces,)),
            pltpu.SemaphoreType.DMA,
            pltpu.SemaphoreType.DMA((2,)),
            pltpu.SemaphoreType.DMA((2,)),
        ],
        compiler_params=pltpu.CompilerParams(
            collective_id=0, has_side_effects=True, vmem_limit_bytes=need + (4 << 20)
        ),
        cost_estimate=pl.CostEstimate(
            flops=2 * height * panels * width * size**3, bytes_accessed=1 << 28, transcendentals=0
        ),
        name="square",
    )(index, codes, owned, first)[0]


def shards(owned_blocks, slot_rows, block_cols):
    own_slots, panels, size, _ = owned_blocks.shape
    rows = lax.axis_size("row")
    cols = lax.axis_size("col")
    layers = lax.axis_size("layer")
    width = panels // cols
    slots = own_slots * rows * cols * layers
    my_row, my_col, my_layer = (lax.axis_index(a) for a in ("row", "col", "layer"))
    my_group = my_row * layers + my_layer

    ids = jnp.concatenate([slot_rows[:, None], block_cols], axis=1)
    ids = jnp.pad(ids, ((0, -own_slots % 8), (0, -(panels + 1) % 128)))
    ids = meet(ids, rows, cols, layers)[..., :own_slots, : panels + 1].reshape(slots, panels + 1)
    tall = size * FIRST // 128
    first = owned_blocks.reshape(own_slots, cols, width, size, size)[:, :, 0, :tall]
    first, ids = lax.optimization_barrier((first, ids))
    first = lax.all_to_all(first, "col", split_axis=1, concat_axis=0, tiled=True)
    first = first.reshape(cols * own_slots, tall, size)

    nb = NB
    per_layer = panels // (cols * layers) * (nb // panels)
    height = nb // (rows * layers)
    place = jnp.arange(nb, dtype=jnp.int32)
    part, within = place // height, place % height
    row_at = (
        part // layers * (nb // rows)
        + within // per_layer * per_layer * layers
        + part % layers * per_layer
        + within % per_layer
    )
    holds = ids[None, :, 0] == row_at[:, None]
    slot_at = jnp.sum(
        jnp.where(holds, jnp.arange(slots, dtype=jnp.int32)[None, :], 0), axis=1
    )
    my_slots = lax.dynamic_slice_in_dim(slot_at, my_group * height, height)
    owner = my_slots // own_slots // layers % cols
    index = owner * own_slots + my_slots % own_slots

    columns = jnp.dot(
        holds.astype(jnp.float32),
        ids[:, 1:].astype(jnp.float32),
        precision=lax.Precision.HIGHEST,
    ).astype(jnp.int32)
    mine = lax.dynamic_slice_in_dim(columns, my_group * height, height)
    wanted = lax.dynamic_slice_in_dim(mine, my_col * width, width, 1)
    inside = mine % (nb // rows)
    partner = (
        (mine // (nb // rows) * layers + inside // per_layer % layers) * height
        + inside // (per_layer * layers) * per_layer
        + inside % per_layer
    )
    reach = lax.dynamic_slice_in_dim(columns, my_col * width, width, 1)
    matched = reach[partner] == wanted[:, None, :]
    codes = jnp.where(matched, partner[:, :, None], nb).transpose(0, 2, 1)
    return square(index, codes.reshape(-1), owned_blocks, first, rows, cols, layers, height)


def solution(mesh):
    return jax.shard_map(
        shards,
        mesh=mesh,
        in_specs=(
            P(("row", "col", "layer"), None, None, None),
            P(("row", "col", "layer")),
            P(("row", "col", "layer"), None),
        ),
        out_specs=P(("row", "layer"), "col", None, None),
        check_vma=False,
    )
```

```python
import functools

import jax
import jax.numpy as jnp
from jax import lax
from jax.experimental import pallas as pl
from jax.experimental.pallas import tpu as pltpu
from jax.sharding import PartitionSpec as P

MESH = pl.DeviceIdType.MESH
NB = 256
GROUP = 4
FIRST = 64
CUT = 1
SHARE = (1, 1, 1, 1, 1)
EARLY = 3
STRAIGHT = 3


def meet_kernel(rows, cols, layers, mine_ref, all_ref, send_sem, recv_sem):
    my_row, my_col, my_layer = (lax.axis_index(a) for a in ("row", "col", "layer"))
    row_peers = [lax.rem(my_row + d, rows) for d in range(1, rows)]
    col_peers = [lax.rem(my_col + d, cols) for d in range(1, cols)]
    layer_peers = [lax.rem(my_layer + d, layers) for d in range(1, layers)]
    barrier = pltpu.get_barrier_semaphore()
    for axis, peers in (("col", col_peers), ("row", row_peers), ("layer", layer_peers)):
        for peer in peers:
            pl.semaphore_signal(barrier, inc=1, device_id={axis: peer}, device_id_type=MESH)
    all_ref[my_row, my_col, my_layer] = mine_ref[...]
    pl.semaphore_wait(barrier, rows + cols + layers - 3)
    steps = (
        ("layer", layer_peers, my_layer, lambda at: all_ref.at[my_row, my_col, at]),
        ("row", row_peers, my_row, lambda at: all_ref.at[at, my_col]),
        ("col", col_peers, my_col, lambda at: all_ref.at[:, at]),
    )
    sent = 0
    for axis, peers, me, place in steps:

        def copy(n, peer, at, place=place, axis=axis, base=sent):
            return pltpu.make_async_remote_copy(
                src_ref=place(at),
                dst_ref=place(at),
                send_sem=send_sem.at[base + n],
                recv_sem=recv_sem.at[base + n],
                device_id={axis: peer},
                device_id_type=MESH,
            )

        copies = [copy(n, peer, me) for n, peer in enumerate(peers)]
        for one in copies:
            one.start()
        size = len(peers) + 1
        for n in range(len(peers)):
            copy(n, peers[n], lax.rem(me + size - n - 1, size)).wait_recv()
        for one in copies:
            one.wait_send()
        sent += len(peers)


def meet(mine, rows, cols, layers):
    count = rows + cols + layers - 3
    return pl.pallas_call(
        functools.partial(meet_kernel, rows, cols, layers),
        out_shape=jax.ShapeDtypeStruct((rows, cols, layers) + mine.shape, mine.dtype),
        in_specs=[pl.BlockSpec(memory_space=pltpu.VMEM)],
        out_specs=pl.BlockSpec(memory_space=pltpu.VMEM),
        scratch_shapes=[
            pltpu.SemaphoreType.DMA((count,)),
            pltpu.SemaphoreType.DMA((count,)),
        ],
        compiler_params=pltpu.CompilerParams(collective_id=1, has_side_effects=True),
        name="meet",
    )(mine)


def square_kernel(
    rows, cols, layers, outer, parts, chunks, index_ref, code_ref, owned_ref, first_ref,
    out_ref, left_ref, land_ref, *scratch,
):
    width, _, height = left_ref.shape[:3]
    slots = owned_ref.shape[0]
    panels = cols * width
    nb = rows * layers * height
    tables = scratch[:width]
    (
        got, sums, a_buf, o_buf, swap_send, swap_recv, send_sem, recv_sem, row_send,
        layer_send, table_recv, own_sem, got_sem, a_sem, o_sem,
    ) = scratch[width:]
    inner = cols // outer
    my_row, my_col, my_layer = (lax.axis_index(a) for a in ("row", "col", "layer"))
    my_outer, my_inner = my_col // inner, lax.rem(my_col, inner)
    my_group = my_row * layers + my_layer

    row_peers = [lax.rem(my_row + d, rows) for d in range(1, rows)]
    layer_peers = [lax.rem(my_layer + d, layers) for d in range(1, layers)]
    far_first = sorted(range(1, cols), key=lambda d: abs(2 * d - cols))
    col_peers = [lax.rem(my_col + d, cols) for d in far_first]
    col_givers = [lax.rem(my_col + cols - d, cols) for d in far_first]
    barrier = pltpu.get_barrier_semaphore()
    for axis, peers in (("col", col_peers), ("row", row_peers), ("layer", layer_peers)):
        for peer in peers:
            pl.semaphore_signal(barrier, inc=1, device_id={axis: peer}, device_id_type=MESH)
    pl.semaphore_wait(barrier, rows + cols + layers - 3)

    def swap(n, d):
        q, low, tall = chunks[n]
        return pltpu.make_async_remote_copy(
            src_ref=owned_ref.at[:, col_peers[d - 1] * width + q, pl.ds(low, tall)],
            dst_ref=land_ref.at[q, pl.ds(my_col * slots, slots), pl.ds(low, tall)],
            send_sem=swap_send.at[n, d],
            recv_sem=swap_recv.at[n, my_col],
            device_id={"col": col_peers[d - 1]},
            device_id_type=MESH,
        )

    def keep(n):
        q, low, tall = chunks[n]
        return pltpu.make_async_copy(
            owned_ref.at[:, my_col * width + q, pl.ds(low, tall)],
            land_ref.at[q, pl.ds(my_col * slots, slots), pl.ds(low, tall)],
            swap_send.at[n, 0],
        )

    def start_swap(n):
        if n < len(chunks):
            keep(n).start()
            for d in range(1, cols):
                swap(n, d).start()

    def wait_swap(n):
        q, low, tall = chunks[n]
        keep(n).wait()
        for giver in col_givers:
            place = land_ref.at[q, pl.ds(giver * slots, slots), pl.ds(low, tall)]
            pltpu.make_async_remote_copy(
                src_ref=place,
                dst_ref=place,
                send_sem=swap_send.at[n, 1],
                recv_sem=swap_recv.at[n, giver],
                device_id={"col": giver},
                device_id_type=MESH,
            ).wait_recv()

    lines = (
        (my_outer + 1 < outer, {"col": my_col + inner}),
        (my_outer >= 1, {"col": my_col - inner}),
        (my_inner + 1 < inner, {"col": my_col + 1}),
        (my_inner >= 1, {"col": my_col - 1}),
    )
    ending = []

    def left_place(n, kind, item):
        q, low, tall = chunks[n]
        start, size, _ = parts[n][kind]
        return left_ref.at[q, item, pl.ds(start, size), pl.ds(low, tall)]

    def send_left(n, kind, item, way, condition, own=False):
        q, low, tall = chunks[n]
        start, size, _ = parts[n][kind]

        def make():
            place = left_place(n, kind, item)
            source = place
            if own:
                source = tables[q].at[pl.ds(my_group * height + start, size), pl.ds(low, tall)]
            return pltpu.make_async_remote_copy(
                src_ref=source,
                dst_ref=place,
                send_sem=send_sem.at[n, kind, item, way],
                recv_sem=recv_sem.at[n, kind, item],
                device_id=lines[way][1],
                device_id_type=MESH,
            )

        condition = jnp.logical_and(condition, lines[way][0])

        @pl.when(condition)
        def _():
            make().start()

        ending.append((condition, make))

    def wait_left(n, kind, item, condition):
        @pl.when(condition)
        def _():
            place = left_place(n, kind, item)
            pltpu.make_async_remote_copy(
                src_ref=place,
                dst_ref=place,
                send_sem=send_sem.at[n, kind, item, 0],
                recv_sem=recv_sem.at[n, kind, item],
                device_id={"col": my_col},
                device_id_type=MESH,
            ).wait_recv()

    always = my_col >= 0
    axes = (
        (outer, inner, my_outer, (0, 1)),
        (inner, 1, my_inner, (2, 3)),
    )

    def stages(n, kind, first, second):
        size1, stride1, me1, ways1 = first
        size2, stride2, me2, ways2 = second

        def own():
            for way in ways1 + ways2:
                send_left(n, kind, my_col, way, always, own=True)

        def along_first(step):
            for sign, way in ((-1, ways1[0]), (1, ways1[1])):
                at = me1 + sign * step
                there = at >= 0 if sign < 0 else at < size1
                item = at * stride1 + me2 * stride2
                wait_left(n, kind, item, there)
                for onward in (way,) + ways2:
                    send_left(n, kind, item, onward, there)

        def along_second(step):
            for sign, way in ((-1, ways2[0]), (1, ways2[1])):
                at = me2 + sign * step
                there = at >= 0 if sign < 0 else at < size2
                for other in range(size1):
                    item = other * stride1 + at * stride2
                    wait_left(n, kind, item, there)
                    send_left(n, kind, item, way, there)

        return (
            [own]
            + [functools.partial(along_first, s) for s in range(1, size1)]
            + [functools.partial(along_second, s) for s in range(1, size2)]
        )

    plans = [
        [
            stages(n, kind, *(axes if part[2] else axes[::-1]))
            for kind, part in enumerate(parts[n])
        ]
        for n in range(len(chunks))
    ]
    depth = len(plans[0][0])

    def table_copy(n, group, sem, device):
        q, low, tall = chunks[n]
        place = tables[q].at[pl.ds(group * height, height), pl.ds(low, tall)]
        return pltpu.make_async_remote_copy(
            src_ref=place,
            dst_ref=place,
            send_sem=sem,
            recv_sem=table_recv.at[n, group],
            device_id=device,
            device_id_type=MESH,
        )

    def row_copy(n, d):
        return table_copy(n, my_group, row_send.at[n, d], {"row": row_peers[d]})

    def layer_copy(n, d, row):
        group = row * layers + my_layer
        return table_copy(n, group, layer_send.at[n, d, row], {"layer": layer_peers[d]})

    def wait_table(n, group):
        table_copy(n, group, row_send.at[n, 0], {"row": my_row}).wait_recv()

    def own_left(n):
        q, low, tall = chunks[n]
        return pltpu.make_async_copy(
            tables[q].at[pl.ds(my_group * height, height), pl.ds(low, tall)],
            left_ref.at[q, my_col, :, pl.ds(low, tall)],
            own_sem.at[n],
        )

    def arrive(n):
        q, low, tall = chunks[n]
        source = first_ref
        if n:
            wait_swap(n)
            source = land_ref.at[q, :, pl.ds(low, tall)]
            start_swap(n + 1)
        fetch = pltpu.make_async_copy(source, got.at[:, pl.ds(low, tall)], got_sem)
        fetch.start()
        fetch.wait()

        def pick(t, carry):
            tables[q][my_group * height + t, pl.ds(low, tall)] = got[index_ref[t], pl.ds(low, tall)]
            return carry

        lax.fori_loop(0, height, pick, 0)
        for plan in plans[n]:
            plan[0]()
        for d in range(rows - 1):
            row_copy(n, d).start()
        for d in range(layers - 1):
            layer_copy(n, d, my_row).start()
        own_left(n).start()

    def gather(n, stage):
        for plan in plans[n]:
            plan[stage]()
        if stage == 1:
            for peer in row_peers:
                wait_table(n, peer * layers + my_layer)
                for d in range(layers - 1):
                    layer_copy(n, d, peer).start()

    def fetch(q, i, slot):
        return pltpu.make_async_copy(
            left_ref.at[q, :, pl.ds(i * GROUP, GROUP)], a_buf.at[slot], a_sem.at[slot]
        )

    def put(i, slot):
        return pltpu.make_async_copy(
            o_buf.at[slot], out_ref.at[pl.ds(i * GROUP, GROUP)], o_sem.at[slot]
        )

    def multiply(q, low, high):
        first, last = q == 0, q == width - 1
        low, high = low // GROUP, high // GROUP
        fetch(q, low, low % 2).start()

        def some_rows(i, carry):
            slot = lax.rem(i, 2)

            @pl.when(i + 1 < high)
            def _():
                fetch(q, i + 1, 1 - slot).start()

            if last:

                @pl.when(i >= 2)
                def _():
                    put(i - 2, slot).wait()

            fetch(q, i, slot).wait()

            def one_row(g, carry):
                t = i * GROUP + g
                lefts = jnp.concatenate([a_buf[slot, c, g] for c in range(cols)], axis=1)
                for j in range(width):
                    start = (t * width + j) * panels + q
                    rights = [tables[j][code_ref[start + c * width]] for c in range(cols)]
                    term = jnp.dot(
                        lefts,
                        jnp.concatenate(rights, axis=0),
                        preferred_element_type=jnp.float32,
                    )
                    if not first:
                        term = sums[t, j] + term
                    if last:
                        o_buf[slot, g, j] = term.astype(o_buf.dtype)
                    else:
                        sums[t, j] = term
                return carry

            lax.fori_loop(0, GROUP, one_row, 0)
            if last:
                put(i, slot).start()
            return carry

        lax.fori_loop(low, high, some_rows, 0)

    start_swap(1)
    for q in range(width):
        tables[q][nb] = jnp.zeros_like(tables[q][nb])

    ready = {q: max(n for n, chunk in enumerate(chunks) if chunk[0] == q) for q in range(width)}
    final = len(chunks) - 1
    done = 0
    for turn in range(final + depth - 1):
        for n in range(len(chunks)):
            stage = turn - n
            if stage == 0:
                arrive(n)
            elif 0 < stage < depth:
                gather(n, stage)
        if turn == final + 1:
            for n in range(len(chunks)):
                for layer_peer in layer_peers:
                    for row in range(rows):
                        wait_table(n, row * layers + layer_peer)
                own_left(n).wait()
        if turn > final:
            while done < width - 1 and turn - ready[done] >= depth - 1:
                multiply(done, 0, height)
                done += 1
    while done < width - 1:
        multiply(done, 0, height)
        done += 1
    for kind, (start, size, _) in enumerate(parts[final]):
        plans[final][kind][depth - 1]()
        multiply(width - 1, start, start + size)
    for i in range(max(height // GROUP - 2, 0), height // GROUP):
        put(i, i % 2).wait()

    for condition, make in ending:

        @pl.when(condition)
        def _(make=make):
            make().wait_send()

    for n in range(len(chunks)):
        if n:
            for d in range(1, cols):
                swap(n, d).wait_send()
        for d in range(rows - 1):
            row_copy(n, d).wait_send()
        for d in range(layers - 1):
            for row in [my_row] + row_peers:
                layer_copy(n, d, row).wait_send()


def square(index, codes, owned, first, rows, cols, layers, height):
    slots, panels, size, _ = owned.shape
    width = panels // cols
    nb = rows * layers * height
    outer = 4 if cols % 4 == 0 else 1
    tall = first.shape[1]
    chunks = [(0, low, tall) for low in range(0, size, tall)]
    step = size // CUT
    chunks += [(q, low, step) for q in range(1, width) for low in range(0, size, step)]
    pieces = len(chunks)
    blocks = height // GROUP
    parts = []
    for n in range(pieces):
        share = SHARE[n * len(SHARE) // pieces]
        straight = STRAIGHT if n == pieces - 1 else EARLY
        swapped = blocks * share // 16
        cuts = [swapped + (blocks - swapped) * k // straight for k in range(straight + 1)]
        parts.append(((0, swapped * GROUP, False),) * (swapped > 0) + tuple(
            (lo * GROUP, (hi - lo) * GROUP, True) for lo, hi in zip(cuts, cuts[1:])
        ))
    kinds = max(len(part) for part in parts)
    kind = owned.dtype
    scratch = [pltpu.VMEM((nb + 1, size, size), kind) for _ in range(width)] + [
        pltpu.VMEM((cols * slots, size, size), kind),
        pltpu.VMEM((height, width, size, size), jnp.float32),
        pltpu.VMEM((2, cols, GROUP, size, size), kind),
        pltpu.VMEM((2, GROUP, width, size, size), kind),
    ]
    need = sum(s.shape[0] * jnp.dtype(s.dtype).itemsize * (
        functools.reduce(lambda a, b: a * b, s.shape[1:])) for s in scratch)
    anywhere = pl.BlockSpec(memory_space=pl.ANY)
    return pl.pallas_call(
        functools.partial(square_kernel, rows, cols, layers, outer, tuple(parts), tuple(chunks)),
        out_shape=(
            jax.ShapeDtypeStruct((height, width, size, size), kind),
            jax.ShapeDtypeStruct((width, cols, height, size, size), kind),
            jax.ShapeDtypeStruct((width, cols * slots, size, size), kind),
        ),
        in_specs=[pl.BlockSpec(memory_space=pltpu.SMEM)] * 2 + [anywhere] * 2,
        out_specs=(anywhere,) * 3,
        scratch_shapes=scratch + [
            pltpu.SemaphoreType.DMA((pieces, cols)),
            pltpu.SemaphoreType.DMA((pieces, cols)),
            pltpu.SemaphoreType.DMA((pieces, kinds, cols, 4)),
            pltpu.SemaphoreType.DMA((pieces, kinds, cols)),
            pltpu.SemaphoreType.DMA((pieces, max(rows - 1, 1))),
            pltpu.SemaphoreType.DMA((pieces, max(layers - 1, 1), rows)),
            pltpu.SemaphoreType.DMA((pieces, rows * layers)),
            pltpu.SemaphoreType.DMA((pieces,)),
            pltpu.SemaphoreType.DMA,
            pltpu.SemaphoreType.DMA((2,)),
            pltpu.SemaphoreType.DMA((2,)),
        ],
        compiler_params=pltpu.CompilerParams(
            collective_id=0, has_side_effects=True, vmem_limit_bytes=need + (4 << 20)
        ),
        cost_estimate=pl.CostEstimate(
            flops=2 * height * panels * width * size**3, bytes_accessed=1 << 28, transcendentals=0
        ),
        name="square",
    )(index, codes, owned, first)[0]


def shards(owned_blocks, slot_rows, block_cols):
    own_slots, panels, size, _ = owned_blocks.shape
    rows = lax.axis_size("row")
    cols = lax.axis_size("col")
    layers = lax.axis_size("layer")
    width = panels // cols
    slots = own_slots * rows * cols * layers
    my_row, my_col, my_layer = (lax.axis_index(a) for a in ("row", "col", "layer"))
    my_group = my_row * layers + my_layer

    ids = jnp.concatenate([slot_rows[:, None], block_cols], axis=1)
    ids = jnp.pad(ids, ((0, -own_slots % 8), (0, -(panels + 1) % 128)))
    ids = meet(ids, rows, cols, layers)[..., :own_slots, : panels + 1].reshape(slots, panels + 1)
    tall = size * FIRST // 128
    first = owned_blocks.reshape(own_slots, cols, width, size, size)[:, :, 0, :tall]
    first, ids = lax.optimization_barrier((first, ids))
    first = lax.all_to_all(first, "col", split_axis=1, concat_axis=0, tiled=True)
    first = first.reshape(cols * own_slots, tall, size)

    nb = NB
    per_layer = panels // (cols * layers) * (nb // panels)
    height = nb // (rows * layers)
    place = jnp.arange(nb, dtype=jnp.int32)
    part, within = place // height, place % height
    row_at = (
        part // layers * (nb // rows)
        + within // per_layer * per_layer * layers
        + part % layers * per_layer
        + within % per_layer
    )
    holds = ids[None, :, 0] == row_at[:, None]
    slot_at = jnp.sum(
        jnp.where(holds, jnp.arange(slots, dtype=jnp.int32)[None, :], 0), axis=1
    )
    my_slots = lax.dynamic_slice_in_dim(slot_at, my_group * height, height)
    owner = my_slots // own_slots // layers % cols
    index = owner * own_slots + my_slots % own_slots

    columns = jnp.dot(
        holds.astype(jnp.float32),
        ids[:, 1:].astype(jnp.float32),
        precision=lax.Precision.HIGHEST,
    ).astype(jnp.int32)
    mine = lax.dynamic_slice_in_dim(columns, my_group * height, height)
    wanted = lax.dynamic_slice_in_dim(mine, my_col * width, width, 1)
    inside = mine % (nb // rows)
    partner = (
        (mine // (nb // rows) * layers + inside // per_layer % layers) * height
        + inside // (per_layer * layers) * per_layer
        + inside % per_layer
    )
    reach = lax.dynamic_slice_in_dim(columns, my_col * width, width, 1)
    matched = reach[partner] == wanted[:, None, :]
    codes = jnp.where(matched, partner[:, :, None], nb).transpose(0, 2, 1)
    return square(index, codes.reshape(-1), owned_blocks, first, rows, cols, layers, height)


def solution(mesh):
    return jax.shard_map(
        shards,
        mesh=mesh,
        in_specs=(
            P(("row", "col", "layer"), None, None, None),
            P(("row", "col", "layer")),
            P(("row", "col", "layer"), None),
        ),
        out_specs=P(("row", "layer"), "col", None, None),
        check_vma=False,
    )
```
